512 devices in a mesh: dp: 16 (over y, core), tensor: 32 (over x, z).
Axes of the slice: x: 4, y: 8, z: 8, core: 2. Of those that a mesh axis runs over, the one named last changes fastest.
Arguments:
- tokens: bfloat16 [32768, 2048], P(('dp', 'tensor')), may hold values from -6 to 6
- norm_gain: bfloat16 [2048], replicated, may hold values from 0.25 to 1.75
- query_weight: bfloat16 [2048, 2048], P('dp'), may hold values from -0.125 to 0.125
- keyval_weight: bfloat16 [2, 2048, 512], P(None, 'dp'), may hold values from -0.125 to 0.125
- query_gain: float32 [64], replicated, may hold values from 0.5 to 2
- key_gain: float32 [64], replicated, may hold values from 0.5 to 2
- output_weight: bfloat16 [2048, 2048], P(None, 'dp'), may hold values from -0.75 to 0.75
- keyval_cache: bfloat16 [512, 2048, 128], P(('dp', 'tensor')), may hold values from -96 to 96
- cached_lengths: int32 [64], P('dp'), may hold values from 1 to 2048, as said below
- sink_count: int32 [64], P('dp'), may hold values from 1 to 32
- window: int32 [64], P('dp'), may hold values from 512 to 4096, as said below
Outputs:
- attended: bfloat16 [32768, 2048], P(('dp', 'tensor'))
- fresh_keyvals: bfloat16 [512, 512, 128], P(('dp', 'tensor'))
The draws below stay inside these ranges and needn't reach their ends.
Inputs may be any that keep to these rules, and one draw needn't show every extreme that they name: `cached_lengths`: some request has exactly 2048 cached tokens. Some request has a window of exactly 4096.
All inputs are finite; a program needn't handle non-finite values.
Results may differ from the reference program's by a relative error of at most 0.014.
The reference program's roundings to bfloat16 on the way count: a program that leaves them out, or rounds other values in their place, can miss the bound.
Values may be sent and summed in bfloat16 or wider, within the bound.
A program may use at most 64 MiB of HBM per device.

```python
import math
import jax
import jax.numpy as jnp
from jax import lax

D = 2048
HEADS = 32
KVH = 8
HD = 64
NEW = 512
CACHE = 2048
WINDOW = 4096
REQS = 64


def draw_cached_lengths(key, part):
    first_key, second_key = jax.random.split(jax.random.fold_in(key, 11))
    lengths = jax.random.randint(first_key, (REQS,), 1, CACHE + 1)
    chosen = jax.random.randint(second_key, (), 0, REQS)
    return jnp.where(jnp.arange(REQS) == chosen, CACHE, lengths).astype(jnp.int32)


def draw_window(key, part):
    first_key, second_key = jax.random.split(jax.random.fold_in(key, 23))
    widths = jax.random.randint(first_key, (REQS,), WINDOW // 8, WINDOW + 1)
    chosen = jax.random.randint(second_key, (), 0, REQS)
    return jnp.where(jnp.arange(REQS) == chosen, WINDOW, widths).astype(jnp.int32)


def draw_keyval_cache(key, part):
    parts_keys = jax.random.split(jax.random.fold_in(key, 37), 6)
    shape = (REQS * KVH, CACHE, 2 * HD)
    return jnp.clip(jax.random.normal(parts_keys[5], shape, jnp.float32), -6.0, 6.0).astype(jnp.bfloat16)


def plant(drawn, stream_key, low, high):
    longest = drawn.shape.index(max(drawn.shape))
    spots = []
    for shift in (0, 1):
        where = [jax.random.randint(jax.random.fold_in(stream_key, axis), (), 0, length) for axis, length in enumerate(drawn.shape)]
        where[longest] = (where[longest] + shift) % drawn.shape[longest]
        spots.append(tuple(where))
    return drawn.at[spots[0]].set(low).at[spots[1]].set(high)


def level_of(rng, extent, shards, least, largest):
    level = 1.0
    for position, shards_of in shards:
        draws = jax.random.uniform(jax.random.fold_in(jax.random.fold_in(rng, 6), position), (shards_of,), jnp.float32, least / len(shards), largest / len(shards))
        level = level * jnp.repeat(jnp.exp(draws), extent[position] // shards_of).reshape((-1,) + (1,) * (len(extent) - 1 - position))
    return level


def gaussian(own_key, extent, deviation, reach, cuts=(), kind=jnp.bfloat16):
    factor_of = level_of(own_key, extent, cuts, -0.22, 0.18) if cuts else 1.0
    drawn = jax.random.normal(own_key, extent, jnp.float32) * deviation * factor_of
    return jnp.minimum(jnp.maximum(drawn, -reach), reach).astype(kind)


def setup_inputs(seed: int = 0) -> dict:
    splits = jax.random.split(jax.random.key(seed), 12)
    tokens = gaussian(splits[0], (REQS * NEW, D), 1.0, 6.0, ((0, 512),))
    norm_gain = jnp.clip(1.0 + 0.15 * jax.random.normal(splits[1], (D,), jnp.float32), 0.25, 1.75).astype(jnp.bfloat16)
    query_weight = gaussian(splits[2], (D, HEADS * HD), D ** -0.5, 0.125, ((0, 16),))
    keyval_weight = gaussian(splits[3], (2, D, KVH * HD), D ** -0.5, 0.125, ((1, 16),))
    query_gain = jnp.clip(jnp.exp(jax.random.uniform(splits[4], (HD,), jnp.float32, math.log(0.5), math.log(2.0))), 0.5, 2.0)
    key_gain = jnp.clip(jnp.exp(jax.random.uniform(splits[5], (HD,), jnp.float32, math.log(0.5), math.log(2.0))), 0.5, 2.0)
    output_weight = gaussian(splits[6], (HEADS * HD, D), HD ** -0.5, 0.75, ((1, 16),))
    keyval_cache = draw_keyval_cache(jax.random.fold_in(splits[11], 71), 0)
    cached_lengths = draw_cached_lengths(jax.random.fold_in(splits[11], 71), 0)
    sink_count = plant(jax.random.randint(splits[9], (REQS,), 1, 33), jax.random.fold_in(splits[9], 1), 1, 32).astype(jnp.int32)
    window = draw_window(jax.random.fold_in(splits[11], 71), 0)
    return {"tokens": tokens, "norm_gain": norm_gain, "query_weight": query_weight, "keyval_weight": keyval_weight, "query_gain": query_gain, "key_gain": key_gain, "output_weight": output_weight, "keyval_cache": keyval_cache, "cached_lengths": cached_lengths, "sink_count": sink_count, "window": window}


epsilon = 1e-05
theta_base = 1000000.0

def rms_scale(values, weights):
    mean_square = lax.optimization_barrier(jnp.mean(values * values, axis=-1, keepdims=True))
    return values * lax.rsqrt(mean_square + epsilon) * weights

def rotate(values, positions):
    half_dim = values.shape[-1] // 2
    inverse_freq = theta_base ** (-2.0 * jnp.arange(half_dim, dtype=jnp.float32) / values.shape[-1])
    angles = positions.astype(jnp.float32)[:, None] * inverse_freq[None, :]
    cosine = jnp.cos(angles)
    sine_part = jnp.sin(angles)
    first_half = values[..., :half_dim]
    second_half = values[..., half_dim:]
    return jnp.concatenate([first_half * cosine - second_half * sine_part, second_half * cosine + first_half * sine_part], axis=-1)

def reference(tokens, norm_gain, query_weight, keyval_weight, query_gain, key_gain, output_weight, keyval_cache, cached_lengths, sink_count, window):
    group_size = HEADS // KVH
    scale = HD ** (-0.5)
    request_tokens_all = tokens.reshape(REQS, NEW, D)
    caches = keyval_cache.reshape(REQS, KVH, CACHE, 2 * HD)

    def one_request(operands):
        request_tokens, request_cache, length, sink_total, window_len = operands
        normed = rms_scale(request_tokens.astype(jnp.float32), norm_gain.astype(jnp.float32)).astype(jnp.bfloat16)
        query_raw = jnp.dot(normed, query_weight, preferred_element_type=jnp.float32).reshape(NEW, HEADS, HD).transpose(1, 0, 2)
        key_raw = jnp.dot(normed, keyval_weight[0], preferred_element_type=jnp.float32).reshape(NEW, KVH, HD).transpose(1, 0, 2)
        value_new = jnp.dot(normed, keyval_weight[1], preferred_element_type=jnp.float32).astype(jnp.bfloat16).reshape(NEW, KVH, HD).transpose(1, 0, 2)
        positions = length + jnp.arange(NEW, dtype=jnp.int32)
        queries = rotate(rms_scale(query_raw, query_gain), positions).astype(jnp.bfloat16)
        key_new = rotate(rms_scale(key_raw, key_gain), positions).astype(jnp.bfloat16)
        fresh_rows = jnp.concatenate([key_new, value_new], axis=2)
        all_keys = jnp.concatenate([request_cache[:, :, :HD], key_new], axis=1)
        all_values = jnp.concatenate([request_cache[:, :, HD:], value_new], axis=1)
        cache_slots = jnp.arange(CACHE, dtype=jnp.int32)
        key_pos = jnp.concatenate([cache_slots, positions])
        key_live = jnp.concatenate([cache_slots < length, jnp.ones((NEW,), jnp.bool_)])
        allowed = key_live[None, :] & (key_pos[None, :] <= positions[:, None]) & ((key_pos[None, :] < sink_total) | (positions[:, None] - key_pos[None, :] < window_len))

        def one_head(head_index):
            keys_here = all_keys[head_index // group_size].astype(jnp.float32)
            values_here = all_values[head_index // group_size].astype(jnp.float32)
            scores = jnp.dot(queries[head_index].astype(jnp.float32), keys_here.T) * scale
            row_max = lax.optimization_barrier(jnp.max(jnp.where(allowed, scores, -jnp.inf), axis=1, keepdims=True))
            weights = jnp.where(allowed, jnp.exp(scores - row_max), 0.0)
            total = lax.optimization_barrier(jnp.sum(weights, axis=1, keepdims=True))
            mixed = jnp.dot(weights.astype(jnp.bfloat16).astype(jnp.float32), values_here)
            return (mixed / total).astype(jnp.bfloat16)
        head_outputs = lax.map(one_head, jnp.arange(HEADS, dtype=jnp.int32))
        joined = head_outputs.transpose(1, 0, 2).reshape(NEW, HEADS * HD)
        attended_rows = jnp.dot(joined, output_weight, preferred_element_type=jnp.float32).astype(jnp.bfloat16)
        return (attended_rows, fresh_rows)
    attended, fresh_keyvals = lax.map(one_request, (request_tokens_all, caches, cached_lengths, sink_count, window))
    return (attended.reshape(REQS * NEW, D), fresh_keyvals.reshape(REQS * KVH, NEW, 2 * HD))
```

```python
import functools

import jax
import jax.numpy as jnp
import numpy as np
from jax import lax
from jax.experimental import pallas as pl
from jax.experimental.pallas import tpu as pltpu
from jax.sharding import PartitionSpec as P

MESH = pl.DeviceIdType.MESH
F32, BF16 = jnp.float32, jnp.bfloat16
epsilon = 1e-05
theta_base = 1000000.0
RING = 8
XS = 4
HD = 64
GROUP = 4
ROWS = 64
NEW = RING * ROWS
CACHE = 2048
D = 2048
QROWS = GROUP * ROWS
SHARD = 128
COLS = 384
KEYS = 512
STAGES = 7
SCALE = float(HD**-0.5 * np.log2(np.e))


def hop_of(stage):
    return stage // 2 + 1 if stage < 6 else 4


def part_of(stage, side):
    return stage % 2 if stage < 6 else side


def next_stage(stage, side):
    if stage <= 3:
        return stage + 2
    return 6 if stage == 4 + side else None


def kernel(
    tokens,
    norm_gain,
    query_weight,
    keyval_weight,
    query_gain,
    key_gain,
    output_weight,
    cache,
    inverse_freq,
    lengths,
    sinks,
    windows,
    out_ref,
    fresh_ref,
    tok,
    w,
    kv_pair,
    wo,
    kc,
    vc,
    new_vc,
    queries,
    accs,
    tops,
    s_ref,
    head_send,
    head_in,
    cos_t,
    sin_t,
    local_sem,
    tok_send,
    tok_recv,
    w_send,
    w_recv,
    wsib_send,
    wsib_recv,
    wo_send,
    wo_recv,
    x_send,
    x_recv,
    wosib_send,
    wosib_recv,
    head_send_sem,
    head_recv_sem,
):
    dp = lax.axis_index("dp")
    rank = lax.axis_index("tensor")
    y, core = dp // 2, dp % 2
    x, z = rank // RING, rank % RING
    parity = x % 2

    def wrap(value, size):
        return (value + size) % size

    def on_z(where):
        return (dp, x * RING + where)

    z_to = [on_z(wrap(z + 1, RING)), on_z(wrap(z - 1, RING))]
    y_to = [(wrap(y + 1, RING) * 2 + core, rank), (wrap(y - 1, RING) * 2 + core, rank)]
    x_to = [(dp, wrap(x + 1, XS) * RING + z), (dp, wrap(x - 1, XS) * RING + z)]
    sibling = (y * 2 + 1 - core, rank)
    step_back = [-1, 1]

    barrier = pltpu.get_barrier_semaphore()
    for apart in range(1, RING):
        pl.semaphore_signal(
            barrier, inc=1, device_id=on_z(wrap(z + apart, RING)), device_id_type=MESH
        )
    for other in y_to + x_to + [sibling]:
        pl.semaphore_signal(barrier, inc=1, device_id=other, device_id_type=MESH)

    def remote(src, dst, send_sem, recv_sem, device):
        return pltpu.make_async_remote_copy(
            src_ref=src,
            dst_ref=dst,
            send_sem=send_sem,
            recv_sem=recv_sem,
            device_id=device,
            device_id_type=MESH,
        )

    own_rows = pl.ds(pl.multiple_of(dp * SHARD, SHARD), SHARD)
    own_cols = pl.ds(pl.multiple_of(dp * SHARD, SHARD), SHARD)
    locals_ = [
        pltpu.make_async_copy(
            query_weight.at[:, pl.ds(pl.multiple_of(z * 256, 256), 256)],
            w.at[own_rows, pl.ds(0, 256)],
            local_sem.at[0],
        ),
        pltpu.make_async_copy(
            keyval_weight.at[:, :, pl.ds(pl.multiple_of(z // 2 * 128, 128), 128)],
            kv_pair,
            local_sem.at[1],
        ),
        pltpu.make_async_copy(cache.at[0], kc, local_sem.at[2]),
        pltpu.make_async_copy(
            tokens, tok.at[pl.ds(pl.multiple_of(z * ROWS, ROWS), ROWS)], local_sem.at[3]
        ),
        pltpu.make_async_copy(output_weight, wo.at[:, own_cols], local_sem.at[4]),
    ]
    for copy in locals_:
        copy.start()

    lane = lax.broadcasted_iota(jnp.int32, (1, 128), 1)
    low = lane < HD

    locals_[1].wait()
    odd = z % 2 == 1
    pair = kv_pair[...].astype(F32)
    key_cols = jnp.where(odd, pltpu.roll(pair[0], HD, 1), pair[0])
    value_cols = jnp.where(odd, pair[1], pltpu.roll(pair[1], HD, 1))
    w[own_rows, 256:384] = jnp.where(low, key_cols, value_cols).astype(BF16)
    locals_[0].wait()

    pl.semaphore_wait(barrier, RING - 1 + 5)

    def tok_rows(block, part):
        return pl.ds(pl.multiple_of(block * ROWS + part * 32, 32), 32)

    def tok_copy(side, stage, block, src=None):
        rows = tok_rows(block, part_of(stage, side))
        return remote(
            tok.at[rows] if src is None else src,
            tok.at[rows],
            tok_send.at[side],
            tok_recv.at[side, stage],
            z_to[side],
        )

    def tok_pump(stage):
        for side in range(2):
            block = wrap(z + step_back[side] * hop_of(stage), RING)
            tok_copy(side, stage, block).wait_recv()
            later = next_stage(stage, side)
            if later is not None:
                tok_copy(side, later, block).start()

    def w_rows(shard, part):
        return pl.ds(pl.multiple_of(shard * SHARD + part * 64, 64), 64)

    def w_copy(side, stage, shard):
        rows = w_rows(shard, part_of(stage, side))
        return remote(
            w.at[rows], w.at[rows], w_send.at[side], w_recv.at[side, stage], y_to[side]
        )

    def w_pump(stage):
        for side in range(2):
            shard = wrap(y + step_back[side] * hop_of(stage), RING) * 2 + core
            w_copy(side, stage, shard).wait_recv()
            later = next_stage(stage, side)
            if later is not None:
                w_copy(side, later, shard).start()
            rows = w_rows(shard, part_of(stage, side))
            remote(w.at[rows], w.at[rows], wsib_send, wsib_recv, sibling).start()

    def wo_part(shard, first, count):
        return (
            pl.ds(pl.multiple_of(first, 256), count),
            pl.ds(pl.multiple_of(shard * SHARD, SHARD), SHARD),
        )

    def wo_copy(side, stage, shard, from_input=False):
        first = parity * 1024 + part_of(stage, side) * 512
        rows, cols = wo_part(shard, first, 512)
        return remote(
            output_weight.at[rows] if from_input else wo.at[rows, cols],
            wo.at[rows, cols],
            wo_send.at[side],
            wo_recv.at[side, stage],
            y_to[side],
        )

    def wo_sibling(rows, cols):
        remote(wo.at[rows, cols], wo.at[rows, cols], wosib_send, wosib_recv, sibling).start()

    def wo_pump(stage):
        for side in range(2):
            shard = wrap(y + step_back[side] * hop_of(stage), RING) * 2 + core
            wo_copy(side, stage, shard).wait_recv()
            later = next_stage(stage, side)
            if later is not None:
                wo_copy(side, later, shard).start()
            first = parity * 1024 + part_of(stage, side) * 512
            for towards in range(2):
                rows, cols = wo_part(shard, first + towards * 256, 256)
                remote(
                    wo.at[rows, cols],
                    wo.at[rows, cols],
                    x_send.at[towards],
                    x_recv.at[towards, stage],
                    x_to[towards],
                ).start()
            wo_sibling(*wo_part(shard, first, 512))

    def x_pump(stage):
        for towards in range(2):
            both = wo.at[0:512, 0:128]
            remote(
                both, both, x_send.at[towards], x_recv.at[towards, stage], x_to[towards]
            ).wait_recv()
            for side in range(2):
                shard = wrap(y + step_back[side] * hop_of(stage), RING) * 2 + core
                first = (1 - parity) * 1024 + part_of(stage, side) * 512
                wo_sibling(*wo_part(shard, first + towards * 256, 256))

    for stage in range(2):
        for side in range(2):
            w_copy(side, stage, dp).start()
    for stage in range(2):
        for side in range(2):
            tok_copy(side, stage, z, tokens.at[pl.ds(stage * 32, 32)]).start()
    remote(w.at[own_rows], w.at[own_rows], wsib_send, wsib_recv, sibling).start()
    remote(output_weight, wo.at[:, own_cols], wosib_send, wosib_recv, sibling).start()

    length = lengths[x]
    sink_total = sinks[x]
    window = windows[x]
    angle_lane = lax.broadcasted_iota(jnp.int32, (NEW, 128), 1)
    position = (lax.broadcasted_iota(jnp.int32, (NEW, 128), 0) + length).astype(F32)
    angles = position * inverse_freq[...]
    cos_t[...] = jnp.cos(angles)
    sine = jnp.sin(angles)
    sin_t[...] = jnp.where(angle_lane % HD < HD // 2, -sine, sine)

    w_pump(0)
    w_pump(1)
    locals_[2].wait()
    vc[...] = jnp.where(low, jnp.ones((), BF16), kc[...])
    w_pump(2)
    tok_pump(0)
    w_pump(3)
    tok_pump(1)
    w_pump(4)
    w_pump(5)
    for stage in range(2):
        for side in range(2):
            wo_copy(side, stage, dp, True).start()
    w_pump(6)
    locals_[3].wait()
    half_w = w.at[0 : D // 2]
    remote(half_w, half_w, wsib_send, wsib_recv, sibling).wait_recv()

    slot = lax.broadcasted_iota(jnp.int32, (1, CACHE), 1)
    far = 1 << 20
    slot_pos = jnp.where(slot < length, jnp.where(slot < sink_total, far, slot), -far)
    row_token = lax.broadcasted_iota(jnp.int32, (QROWS, 1), 0) % ROWS

    same_head = (
        lax.broadcasted_iota(jnp.int32, (128, 128), 0) // HD
        == lax.broadcasted_iota(jnp.int32, (128, 128), 1) // HD
    )
    averaging = jnp.where(same_head, 1.0 / HD, 0.0).astype(BF16)
    gain = norm_gain[...].astype(F32)
    gain_q = jnp.concatenate([query_gain[...], query_gain[...]], axis=1)
    gain_k = jnp.concatenate([key_gain[...], key_gain[...]], axis=1)
    first_half = lane % HD < HD // 2

    def normed_rotated(tile, gains, cosine, sine):
        square = tile * tile
        upper = square.astype(BF16)
        lower = (square - upper.astype(F32)).astype(BF16)
        mean = jnp.dot(upper, averaging, preferred_element_type=F32) + jnp.dot(
            lower, averaging, preferred_element_type=F32
        )
        scaled = tile * lax.rsqrt(mean + epsilon) * gains
        swapped = jnp.where(
            first_half, pltpu.roll(scaled, 128 - HD // 2, 1), pltpu.roll(scaled, HD // 2, 1)
        )
        return scaled * cosine + swapped * sine

    def project(block):
        rows = pl.ds(pl.multiple_of(block * ROWS, ROWS), ROWS)
        values = tok[rows].astype(F32)
        mean = jnp.mean(values * values, axis=1, keepdims=True)
        normed = (values * lax.rsqrt(mean + epsilon) * gain).astype(BF16)
        raw = jnp.dot(normed, w[...], preferred_element_type=F32)
        cosine, sine = cos_t[rows], sin_t[rows]
        query_rows = pl.multiple_of(block * QROWS, QROWS)
        for pair_index in range(2):
            tile = normed_rotated(
                raw[:, pair_index * 128 : pair_index * 128 + 128], gain_q, cosine, sine
            )
            for odd_head in range(2):
                head = jnp.where(low, pltpu.roll(tile, HD, 1) if odd_head else tile, 0.0)
                at = query_rows + (pair_index * 2 + odd_head) * ROWS
                queries[pl.ds(pl.multiple_of(at, ROWS), ROWS)] = head.astype(BF16)
        last = raw[:, 256:384]
        keyval = jnp.where(low, normed_rotated(last, gain_k, cosine, sine), last).astype(BF16)
        fresh_ref[0, rows] = keyval
        new_vc[rows] = jnp.where(low, jnp.ones((), BF16), keyval)

    def scores_of(block_queries, keys):
        return lax.dot_general(
            block_queries, keys, (((1,), (1,)), ((), ())), preferred_element_type=F32
        )

    def attend_cache(block):
        rows = pl.ds(pl.multiple_of(block * QROWS, QROWS), QROWS)
        block_queries = queries[rows]
        oldest = length + block * ROWS + row_token - window
        top = None
        for low_key in range(0, CACHE, KEYS):
            keys = pl.ds(low_key, KEYS)
            scores = scores_of(block_queries, kc[keys])
            scores = jnp.where(slot_pos[:, low_key : low_key + KEYS] > oldest, scores, -jnp.inf)
            s_ref[:, keys] = scores
            for part in range(0, KEYS, 128):
                piece = scores[:, part : part + 128]
                top = piece if top is None else jnp.maximum(top, piece)
        top = jnp.max(top, axis=1, keepdims=True)
        acc = jnp.zeros((QROWS, 128), F32)
        for low_key in range(0, CACHE, KEYS):
            keys = pl.ds(low_key, KEYS)
            weights = jnp.exp2((s_ref[:, keys] - top) * SCALE).astype(BF16)
            acc = acc + jnp.dot(weights, vc[keys], preferred_element_type=F32)
        accs[rows] = acc
        tops[rows] = jnp.broadcast_to(top, (QROWS, 128))

    new_slot = lax.broadcasted_iota(jnp.int32, (1, NEW), 1)

    def finish(block):
        rows = pl.ds(pl.multiple_of(block * QROWS, QROWS), QROWS)
        scores = scores_of(queries[rows], fresh_ref[0])
        scores = jnp.where(new_slot <= block * ROWS + row_token, scores, -jnp.inf)
        old_top = tops[rows][:, :1]
        top = jnp.maximum(old_top, jnp.max(scores, axis=1, keepdims=True))
        weights = jnp.exp2((scores - top) * SCALE).astype(BF16)
        acc = accs[rows] * jnp.exp2((old_top - top) * SCALE) + jnp.dot(
            weights, new_vc[...], preferred_element_type=F32
        )
        mixed = acc / pltpu.roll(acc, HD, 1)
        tiles = []
        for pair_index in range(2):
            even = mixed[pair_index * 128 : pair_index * 128 + ROWS]
            odd_one = mixed[pair_index * 128 + ROWS : pair_index * 128 + 128]
            tiles.append(jnp.where(low, pltpu.roll(even, HD, 1), odd_one).astype(BF16))
        return tiles

    def block_at(order):
        hop = (order + 1) // 2
        return wrap(z + jnp.where(order % 2 == 1, -hop, hop), RING)

    def one_block(order, unused):
        for stage in range(2, STAGES):
            pl.when(order == stage - 1)(functools.partial(tok_pump, stage))
        for stage in range(4):
            pl.when(order == stage + 3)(functools.partial(wo_pump, stage))
        for stage in range(2):
            pl.when(order == stage + 5)(functools.partial(x_pump, stage))
        block = block_at(order)
        project(block)
        attend_cache(block)
        return unused

    lax.fori_loop(0, RING, one_block, 0)

    own_head = pl.ds(pl.multiple_of(z * 256, 256), 256)

    def head_copy(block):
        rows = pl.ds(pl.multiple_of(block * ROWS, ROWS), ROWS)
        return remote(
            head_send.at[rows], head_in.at[:, own_head], head_send_sem, head_recv_sem, on_z(block)
        )

    def finish_block(index, unused):
        order = RING - 1 - index
        block = block_at(order)
        tiles = finish(block)
        rows = pl.ds(pl.multiple_of(block * ROWS, ROWS), ROWS)
        for pair_index in range(2):
            head_send[rows, pair_index * 128 : pair_index * 128 + 128] = tiles[pair_index]

        @pl.when(order < RING - 1)
        def _():
            head_copy(block_at(order + 1)).start()

        return unused

    lax.fori_loop(0, RING, finish_block, 0)
    head_in[:, own_head] = head_send[pl.ds(pl.multiple_of(z * ROWS, ROWS), ROWS)]
    for stage in range(4, STAGES):
        wo_pump(stage)
        x_pump(stage - 2)
    x_pump(5)
    x_pump(6)
    locals_[4].wait()
    half_wo = wo.at[:, 0 : D // 2]
    remote(half_wo, half_wo, wosib_send, wosib_recv, sibling).wait_recv()
    heads = head_in.at[:, 0 : D - 256]
    remote(heads, heads, head_send_sem, head_recv_sem, sibling).wait_recv()

    def out_cols(index, unused):
        cols = pl.ds(pl.multiple_of(index * 256, 256), 256)
        out_ref[:, cols] = jnp.dot(
            head_in[...], wo[:, cols], preferred_element_type=F32
        ).astype(BF16)
        return unused

    lax.fori_loop(0, D // 256, out_cols, 0)

    for side in range(2):
        sent = tok.at[0:224]
        remote(sent, sent, tok_send.at[side], tok_recv.at[0, 0], z_to[side]).wait_send()
        sent = w.at[0:448]
        remote(sent, sent, w_send.at[side], w_recv.at[0, 0], y_to[side]).wait_send()
        sent = wo.at[0:1792, 0:256]
        remote(sent, sent, wo_send.at[side], wo_recv.at[0, 0], y_to[side]).wait_send()
        remote(sent, sent, x_send.at[side], x_recv.at[0, 0], x_to[side]).wait_send()
    remote(half_w, half_w, wsib_send, wsib_recv, sibling).wait_send()
    remote(half_wo, half_wo, wosib_send, wosib_recv, sibling).wait_send()
    sent = head_send.at[0:448]
    remote(sent, sent, head_send_sem, head_recv_sem, sibling).wait_send()


def body(
    tokens,
    norm_gain,
    query_weight,
    keyval_weight,
    query_gain,
    key_gain,
    output_weight,
    keyval_cache,
    cached_lengths,
    sink_count,
    window,
):
    frequency = theta_base ** (-2.0 * np.arange(HD // 2) / HD)
    inverse_freq = jnp.asarray(np.tile(frequency, 4)[None], F32)
    anywhere = pl.BlockSpec(memory_space=pl.ANY)
    vmem = pl.BlockSpec(memory_space=pltpu.VMEM)
    smem = pl.BlockSpec(memory_space=pltpu.SMEM)
    dma = pltpu.SemaphoreType.DMA
    return pl.pallas_call(
        kernel,
        out_shape=(
            jax.ShapeDtypeStruct((ROWS, D), BF16),
            jax.ShapeDtypeStruct((1, NEW, 2 * HD), BF16),
        ),
        in_specs=[anywhere, vmem, anywhere, anywhere, vmem, vmem, anywhere, anywhere, vmem]
        + [smem] * 3,
        out_specs=(vmem, vmem),
        scratch_shapes=[
            pltpu.VMEM((NEW, D), BF16),
            pltpu.VMEM((D, COLS), BF16),
            pltpu.VMEM((2, SHARD, 128), BF16),
            pltpu.VMEM((D, D), BF16),
            pltpu.VMEM((CACHE, 128), BF16),
            pltpu.VMEM((CACHE, 128), BF16),
            pltpu.VMEM((NEW, 128), BF16),
            pltpu.VMEM((RING * QROWS, 128), BF16),
            pltpu.VMEM((RING * QROWS, 128), F32),
            pltpu.VMEM((RING * QROWS, 128), F32),
            pltpu.VMEM((QROWS, CACHE), F32),
            pltpu.VMEM((NEW, 256), BF16),
            pltpu.VMEM((ROWS, D), BF16),
            pltpu.VMEM((NEW, 128), F32),
            pltpu.VMEM((NEW, 128), F32),
            dma((5,)),
            dma((2,)),
            dma((2, STAGES)),
            dma((2,)),
            dma((2, STAGES)),
            dma(()),
            dma(()),
            dma((2,)),
            dma((2, STAGES)),
            dma((2,)),
            dma((2, STAGES)),
            dma(()),
            dma(()),
            dma(()),
            dma(()),
        ],
        compiler_params=pltpu.CompilerParams(
            collective_id=0, has_side_effects=True, vmem_limit_bytes=60 << 20
        ),
        name="prefill",
    )(
        tokens,
        norm_gain.reshape(1, D),
        query_weight,
        keyval_weight,
        query_gain.reshape(1, HD),
        key_gain.reshape(1, HD),
        output_weight,
        keyval_cache,
        inverse_freq,
        cached_lengths,
        sink_count,
        window,
    )


def solution(mesh):
    in_specs = (
        P(("dp", "tensor"), None),
        P(),
        P("dp", None),
        P(None, "dp", None),
        P(),
        P(),
        P(None, "dp"),
        P(("dp", "tensor"), None, None),
        P("dp"),
        P("dp"),
        P("dp"),
    )
    out_specs = (P(("dp", "tensor"), None), P(("dp", "tensor"), None, None))
    return jax.shard_map(body, mesh=mesh, in_specs=in_specs, out_specs=out_specs, check_vma=False)
```

```python
import functools

import jax
import jax.numpy as jnp
import numpy as np
from jax import lax
from jax.experimental import pallas as pl
from jax.experimental.pallas import tpu as pltpu
from jax.sharding import PartitionSpec as P

MESH = pl.DeviceIdType.MESH
F32, BF16 = jnp.float32, jnp.bfloat16
epsilon = 1e-05
theta_base = 1000000.0
RING = 8
XS = 4
HD = 64
GROUP = 4
ROWS = 64
NEW = RING * ROWS
CACHE = 2048
D = 2048
QROWS = GROUP * ROWS
SHARD = 128
COLS = 384
KEYS = 512
PARTS = 4
STAGES = 3 * PARTS + PARTS // 2
TOK_PART = ROWS // PARTS
WO_PART = 1024 // PARTS
OFFSETS = ((4,), (3, 5), (2, 6), (1, 7))
SCALE = float(HD**-0.5 * np.log2(np.e))


def hop_of(stage):
    return stage // PARTS + 1 if stage < 3 * PARTS else 4


def part_of(stage, side):
    return stage % PARTS if stage < 3 * PARTS else stage - 3 * PARTS + side * (PARTS // 2)


def next_stage(stage, side):
    if stage < 2 * PARTS:
        return stage + PARTS
    part = stage - 2 * PARTS
    if part < PARTS and part // (PARTS // 2) == side:
        return 3 * PARTS + part - side * (PARTS // 2)
    return None


def kernel(
    tokens,
    norm_gain,
    query_weight,
    keyval_weight,
    query_gain,
    key_gain,
    output_weight,
    cache,
    inverse_freq,
    lengths,
    sinks,
    windows,
    out_ref,
    fresh_ref,
    tok,
    w,
    kv_pair,
    wo,
    kc,
    vc,
    new_vc,
    queries,
    accs,
    tops,
    s_ref,
    head_send,
    head_in,
    cos_t,
    sin_t,
    local_sem,
    tok_send,
    tok_recv,
    w_send,
    w_recv,
    wx_send,
    wx_recv,
    wsib_send,
    wsib_recv,
    wo_send,
    wo_recv,
    x_send,
    x_recv,
    wosib_send,
    wosib_recv,
    head_send_sem,
    head_recv_sem,
):
    dp = lax.axis_index("dp")
    rank = lax.axis_index("tensor")
    y, core = dp // 2, dp % 2
    x, z = rank // RING, rank % RING
    parity = x % 2

    def wrap(value, size):
        return (value + size) % size

    def on_z(where):
        return (dp, x * RING + where)

    z_to = [on_z(wrap(z + 1, RING)), on_z(wrap(z - 1, RING))]
    y_to = [(wrap(y + 1, RING) * 2 + core, rank), (wrap(y - 1, RING) * 2 + core, rank)]
    on_y = [(wrap(y + apart, RING) * 2 + core, rank) for apart in range(1, RING)]
    x_to = [(dp, wrap(x + 1, XS) * RING + z), (dp, wrap(x - 1, XS) * RING + z)]
    sibling = (y * 2 + 1 - core, rank)
    step_back = [-1, 1]

    barrier = pltpu.get_barrier_semaphore()
    for apart in range(1, RING):
        pl.semaphore_signal(
            barrier, inc=1, device_id=on_z(wrap(z + apart, RING)), device_id_type=MESH
        )
    for other in on_y + x_to + [sibling]:
        pl.semaphore_signal(barrier, inc=1, device_id=other, device_id_type=MESH)

    def remote(src, dst, send_sem, recv_sem, device):
        return pltpu.make_async_remote_copy(
            src_ref=src,
            dst_ref=dst,
            send_sem=send_sem,
            recv_sem=recv_sem,
            device_id=device,
            device_id_type=MESH,
        )

    own_rows = pl.ds(pl.multiple_of(dp * SHARD, SHARD), SHARD)
    own_cols = pl.ds(pl.multiple_of(dp * SHARD, SHARD), SHARD)
    locals_ = [
        pltpu.make_async_copy(
            query_weight.at[:, pl.ds(pl.multiple_of(z * 256, 256), 256)],
            w.at[own_rows, pl.ds(0, 256)],
            local_sem.at[0],
        ),
        pltpu.make_async_copy(
            keyval_weight.at[:, :, pl.ds(pl.multiple_of(z // 2 * 128, 128), 128)],
            kv_pair,
            local_sem.at[1],
        ),
        pltpu.make_async_copy(cache.at[0], kc, local_sem.at[2]),
        pltpu.make_async_copy(
            tokens, tok.at[pl.ds(pl.multiple_of(z * ROWS, ROWS), ROWS)], local_sem.at[3]
        ),
        pltpu.make_async_copy(output_weight, wo.at[:, own_cols], local_sem.at[4]),
    ]
    for copy in locals_:
        copy.start()

    lane = lax.broadcasted_iota(jnp.int32, (1, 128), 1)
    low = lane < HD

    locals_[1].wait()
    odd = z % 2 == 1
    pair = kv_pair[...].astype(F32)
    key_cols = jnp.where(odd, pltpu.roll(pair[0], HD, 1), pair[0])
    value_cols = jnp.where(odd, pair[1], pltpu.roll(pair[1], HD, 1))
    w[own_rows, 256:384] = jnp.where(low, key_cols, value_cols).astype(BF16)
    locals_[0].wait()

    pl.semaphore_wait(barrier, 2 * (RING - 1) + 3)

    def tok_rows(block, part):
        return pl.ds(pl.multiple_of(block * ROWS + part * TOK_PART, TOK_PART), TOK_PART)

    def tok_copy(side, stage, block, src=None):
        rows = tok_rows(block, part_of(stage, side))
        return remote(
            tok.at[rows] if src is None else src,
            tok.at[rows],
            tok_send.at[side],
            tok_recv.at[side, stage],
            z_to[side],
        )

    def tok_pump(stage):
        for side in range(2):
            block = wrap(z + step_back[side] * hop_of(stage), RING)
            tok_copy(side, stage, block).wait_recv()
            later = next_stage(stage, side)
            if later is not None:
                tok_copy(side, later, block).start()

    def w_rows(shard, first, count):
        return w.at[pl.ds(pl.multiple_of(shard * SHARD + first, 32), count)]

    def y_shard(offset):
        return wrap(y + offset, RING) * 2 + core

    def w_copy(offset):
        rows = w_rows(dp, parity * 64, 64)
        return remote(
            rows, rows, w_send, w_recv.at[offset - 1], (y_shard(offset), rank)
        )

    def w_sibling(rows):
        remote(rows, rows, wsib_send, wsib_recv, sibling).start()

    def w_pump(group):
        for offset in OFFSETS[group]:
            shard = y_shard(-offset)
            rows = w_rows(shard, parity * 64, 64)
            remote(rows, rows, w_send, w_recv.at[offset - 1], sibling).wait_recv()
            for towards in range(2):
                part = w_rows(shard, parity * 64 + towards * 32, 32)
                remote(
                    part, part, wx_send.at[towards], wx_recv.at[towards, group], x_to[towards]
                ).start()
            w_sibling(rows)

    def wx_pump(group):
        for towards in range(2):
            both = w.at[0 : 32 * len(OFFSETS[group])]
            remote(
                both, both, wx_send.at[towards], wx_recv.at[towards, group], x_to[towards]
            ).wait_recv()
            for offset in OFFSETS[group]:
                w_sibling(w_rows(y_shard(-offset), (1 - parity) * 64 + towards * 32, 32))

    def wo_part(shard, first, count):
        return (
            pl.ds(pl.multiple_of(first, 128), count),
            pl.ds(pl.multiple_of(shard * SHARD, SHARD), SHARD),
        )

    def wo_copy(side, stage, shard, from_input=False):
        first = parity * 1024 + part_of(stage, side) * WO_PART
        rows, cols = wo_part(shard, first, WO_PART)
        return remote(
            output_weight.at[rows] if from_input else wo.at[rows, cols],
            wo.at[rows, cols],
            wo_send.at[side],
            wo_recv.at[side, stage],
            y_to[side],
        )

    def wo_sibling(rows, cols):
        remote(wo.at[rows, cols], wo.at[rows, cols], wosib_send, wosib_recv, sibling).start()

    half = WO_PART // 2

    def wo_pump(pair):
        for stage in (2 * pair, 2 * pair + 1):
            for side in range(2):
                shard = y_shard(step_back[side] * hop_of(stage))
                wo_copy(side, stage, shard).wait_recv()
                later = next_stage(stage, side)
                if later is not None:
                    wo_copy(side, later, shard).start()
                first = parity * 1024 + part_of(stage, side) * WO_PART
                for towards in range(2):
                    rows, cols = wo_part(shard, first + towards * half, half)
                    remote(
                        wo.at[rows, cols],
                        wo.at[rows, cols],
                        x_send.at[towards],
                        x_recv.at[towards, pair],
                        x_to[towards],
                    ).start()
                wo_sibling(*wo_part(shard, first, WO_PART))

    def x_pump(pair):
        for towards in range(2):
            four = wo.at[0 : 4 * half, 0:128]
            remote(
                four, four, x_send.at[towards], x_recv.at[towards, pair], x_to[towards]
            ).wait_recv()
            for stage in (2 * pair, 2 * pair + 1):
                for side in range(2):
                    shard = y_shard(step_back[side] * hop_of(stage))
                    first = (1 - parity) * 1024 + part_of(stage, side) * WO_PART
                    wo_sibling(*wo_part(shard, first + towards * half, half))

    for offsets in OFFSETS:
        for offset in offsets:
            w_copy(offset).start()
    for stage in range(PARTS):
        for side in range(2):
            rows = pl.ds(stage * TOK_PART, TOK_PART)
            tok_copy(side, stage, z, tokens.at[rows]).start()
    w_sibling(w.at[own_rows])
    for stage in range(PARTS):
        for side in range(2):
            wo_copy(side, stage, dp, True).start()
    remote(output_weight, wo.at[:, own_cols], wosib_send, wosib_recv, sibling).start()

    length = lengths[x]
    sink_total = sinks[x]
    window = windows[x]
    angle_lane = lax.broadcasted_iota(jnp.int32, (NEW, 128), 1)
    position = (lax.broadcasted_iota(jnp.int32, (NEW, 128), 0) + length).astype(F32)
    angles = position * inverse_freq[...]
    cos_t[...] = jnp.cos(angles)
    sine = jnp.sin(angles)
    sin_t[...] = jnp.where(angle_lane % HD < HD // 2, -sine, sine)

    locals_[2].wait()
    vc[...] = jnp.where(low, jnp.ones((), BF16), kc[...])
    tok_pump(0)
    w_pump(0)
    tok_pump(1)
    w_pump(1)
    tok_pump(2)
    w_pump(2)
    tok_pump(3)
    w_pump(3)
    wx_pump(0)
    wx_pump(1)
    tok_pump(4)
    wx_pump(2)
    tok_pump(5)
    wx_pump(3)
    locals_[3].wait()
    half_w = w.at[0 : D // 2]
    remote(half_w, half_w, wsib_send, wsib_recv, sibling).wait_recv()

    slot = lax.broadcasted_iota(jnp.int32, (1, CACHE), 1)
    far = 1 << 20
    slot_pos = jnp.where(slot < length, jnp.where(slot < sink_total, far, slot), -far)
    row_token = lax.broadcasted_iota(jnp.int32, (QROWS, 1), 0) % ROWS

    same_head = (
        lax.broadcasted_iota(jnp.int32, (128, 128), 0) // HD
        == lax.broadcasted_iota(jnp.int32, (128, 128), 1) // HD
    )
    averaging = jnp.where(same_head, 1.0 / HD, 0.0).astype(BF16)
    gain = norm_gain[...].astype(F32)
    gain_q = jnp.concatenate([query_gain[...], query_gain[...]], axis=1)
    gain_k = jnp.concatenate([key_gain[...], key_gain[...]], axis=1)
    first_half = lane % HD < HD // 2

    def normed_rotated(tile, gains, cosine, sine):
        square = tile * tile
        upper = square.astype(BF16)
        lower = (square - upper.astype(F32)).astype(BF16)
        mean = jnp.dot(upper, averaging, preferred_element_type=F32) + jnp.dot(
            lower, averaging, preferred_element_type=F32
        )
        scaled = tile * lax.rsqrt(mean + epsilon) * gains
        swapped = jnp.where(
            first_half, pltpu.roll(scaled, 128 - HD // 2, 1), pltpu.roll(scaled, HD // 2, 1)
        )
        return scaled * cosine + swapped * sine

    def project(block):
        rows = pl.ds(pl.multiple_of(block * ROWS, ROWS), ROWS)
        values = tok[rows].astype(F32)
        mean = jnp.mean(values * values, axis=1, keepdims=True)
        normed = (values * lax.rsqrt(mean + epsilon) * gain).astype(BF16)
        raw = jnp.dot(normed, w[...], preferred_element_type=F32)
        cosine, sine = cos_t[rows], sin_t[rows]
        query_rows = pl.multiple_of(block * QROWS, QROWS)
        for pair_index in range(2):
            tile = normed_rotated(
                raw[:, pair_index * 128 : pair_index * 128 + 128], gain_q, cosine, sine
            )
            for odd_head in range(2):
                head = jnp.where(low, pltpu.roll(tile, HD, 1) if odd_head else tile, 0.0)
                at = query_rows + (pair_index * 2 + odd_head) * ROWS
                queries[pl.ds(pl.multiple_of(at, ROWS), ROWS)] = head.astype(BF16)
        last = raw[:, 256:384]
        keyval = jnp.where(low, normed_rotated(last, gain_k, cosine, sine), last).astype(BF16)
        fresh_ref[0, rows] = keyval
        new_vc[rows] = jnp.where(low, jnp.ones((), BF16), keyval)

    def scores_of(block_queries, keys):
        return lax.dot_general(
            block_queries, keys, (((1,), (1,)), ((), ())), preferred_element_type=F32
        )

    def attend_cache(block):
        rows = pl.ds(pl.multiple_of(block * QROWS, QROWS), QROWS)
        block_queries = queries[rows]
        oldest = length + block * ROWS + row_token - window
        top = None
        for low_key in range(0, CACHE, KEYS):
            keys = pl.ds(low_key, KEYS)
            scores = scores_of(block_queries, kc[keys])
            scores = jnp.where(slot_pos[:, low_key : low_key + KEYS] > oldest, scores, -jnp.inf)
            s_ref[:, keys] = scores
            for part in range(0, KEYS, 128):
                piece = scores[:, part : part + 128]
                top = piece if top is None else jnp.maximum(top, piece)
        top = jnp.max(top, axis=1, keepdims=True)
        acc = jnp.zeros((QROWS, 128), F32)
        for low_key in range(0, CACHE, KEYS):
            keys = pl.ds(low_key, KEYS)
            weights = jnp.exp2((s_ref[:, keys] - top) * SCALE).astype(BF16)
            acc = acc + jnp.dot(weights, vc[keys], preferred_element_type=F32)
        accs[rows] = acc
        tops[rows] = jnp.broadcast_to(top, (QROWS, 128))

    new_slot = lax.broadcasted_iota(jnp.int32, (1, NEW), 1)

    def finish(block):
        rows = pl.ds(pl.multiple_of(block * QROWS, QROWS), QROWS)
        scores = scores_of(queries[rows], fresh_ref[0])
        scores = jnp.where(new_slot <= block * ROWS + row_token, scores, -jnp.inf)
        old_top = tops[rows][:, :1]
        top = jnp.maximum(old_top, jnp.max(scores, axis=1, keepdims=True))
        weights = jnp.exp2((scores - top) * SCALE).astype(BF16)
        acc = accs[rows] * jnp.exp2((old_top - top) * SCALE) + jnp.dot(
            weights, new_vc[...], preferred_element_type=F32
        )
        mixed = acc / pltpu.roll(acc, HD, 1)
        tiles = []
        for pair_index in range(2):
            even = mixed[pair_index * 128 : pair_index * 128 + ROWS]
            odd_one = mixed[pair_index * 128 + ROWS : pair_index * 128 + 128]
            tiles.append(jnp.where(low, pltpu.roll(even, HD, 1), odd_one).astype(BF16))
        return tiles

    def block_at(order):
        hop = (order + 1) // 2
        return wrap(z + jnp.where(order % 2 == 1, -hop, hop), RING)

    plan = {
        0: [(tok_pump, 6)],
        2: [(tok_pump, 7)],
        3: [(tok_pump, 8), (wo_pump, 0)],
        5: [(tok_pump, 9)],
        6: [(tok_pump, 10), (wo_pump, 1), (x_pump, 0)],
        8: [(tok_pump, 11)],
        9: [(tok_pump, 12), (wo_pump, 2), (x_pump, 1)],
        11: [(tok_pump, 13)],
        12: [(wo_pump, 3), (x_pump, 2)],
        15: [(wo_pump, 4), (x_pump, 3)],
        18: [(wo_pump, 5), (x_pump, 4)],
        21: [(wo_pump, 6), (x_pump, 5)],
    }

    def run_plan(place, first, last, stride):
        for at, steps in plan.items():
            if first <= at < last and (at - first) % stride == 0:

                @pl.when(place == at)
                def _(steps=steps):
                    for pump, which in steps:
                        pump(which)

    def one_block(order, unused):
        block = block_at(order)
        run_plan(order * 2, 0, 2 * RING, 2)
        project(block)
        run_plan(order * 2 + 1, 1, 2 * RING, 2)
        attend_cache(block)
        return unused

    lax.fori_loop(0, RING, one_block, 0)

    own_head = pl.ds(pl.multiple_of(z * 256, 256), 256)

    def head_copy(block):
        rows = pl.ds(pl.multiple_of(block * ROWS, ROWS), ROWS)
        return remote(
            head_send.at[rows], head_in.at[:, own_head], head_send_sem, head_recv_sem, on_z(block)
        )

    def finish_block(index, unused):
        order = RING - 1 - index
        block = block_at(order)
        run_plan(2 * RING + index, 2 * RING, 3 * RING, 1)
        tiles = finish(block)
        rows = pl.ds(pl.multiple_of(block * ROWS, ROWS), ROWS)
        for pair_index in range(2):
            head_send[rows, pair_index * 128 : pair_index * 128 + 128] = tiles[pair_index]

        @pl.when(order < RING - 1)
        def _():
            head_copy(block_at(order + 1)).start()

        return unused

    lax.fori_loop(0, RING, finish_block, 0)
    head_in[:, own_head] = head_send[pl.ds(pl.multiple_of(z * ROWS, ROWS), ROWS)]
    x_pump(6)
    locals_[4].wait()
    half_wo = wo.at[:, 0 : D // 2]
    remote(half_wo, half_wo, wosib_send, wosib_recv, sibling).wait_recv()
    heads = head_in.at[:, 0 : D - 256]
    remote(heads, heads, head_send_sem, head_recv_sem, sibling).wait_recv()

    def out_cols(index, unused):
        cols = pl.ds(pl.multiple_of(index * 256, 256), 256)
        out_ref[:, cols] = jnp.dot(
            head_in[...], wo[:, cols], preferred_element_type=F32
        ).astype(BF16)
        return unused

    lax.fori_loop(0, D // 256, out_cols, 0)

    for side in range(2):
        sent = tok.at[0:224]
        remote(sent, sent, tok_send.at[side], tok_recv.at[0, 0], z_to[side]).wait_send()
        sent = w.at[0:224]
        remote(sent, sent, wx_send.at[side], wx_recv.at[0, 0], x_to[side]).wait_send()
        sent = wo.at[0:1792, 0:256]
        remote(sent, sent, wo_send.at[side], wo_recv.at[0, 0], y_to[side]).wait_send()
        remote(sent, sent, x_send.at[side], x_recv.at[0, 0], x_to[side]).wait_send()
    sent = w.at[0:448]
    remote(sent, sent, w_send, w_recv.at[0], sibling).wait_send()
    remote(half_w, half_w, wsib_send, wsib_recv, sibling).wait_send()
    remote(half_wo, half_wo, wosib_send, wosib_recv, sibling).wait_send()
    sent = head_send.at[0:448]
    remote(sent, sent, head_send_sem, head_recv_sem, sibling).wait_send()


def body(
    tokens,
    norm_gain,
    query_weight,
    keyval_weight,
    query_gain,
    key_gain,
    output_weight,
    keyval_cache,
    cached_lengths,
    sink_count,
    window,
):
    frequency = theta_base ** (-2.0 * np.arange(HD // 2) / HD)
    inverse_freq = jnp.asarray(np.tile(frequency, 4)[None], F32)
    anywhere = pl.BlockSpec(memory_space=pl.ANY)
    vmem = pl.BlockSpec(memory_space=pltpu.VMEM)
    smem = pl.BlockSpec(memory_space=pltpu.SMEM)
    dma = pltpu.SemaphoreType.DMA
    return pl.pallas_call(
        kernel,
        out_shape=(
            jax.ShapeDtypeStruct((ROWS, D), BF16),
            jax.ShapeDtypeStruct((1, NEW, 2 * HD), BF16),
        ),
        in_specs=[anywhere, vmem, anywhere, anywhere, vmem, vmem, anywhere, anywhere, vmem]
        + [smem] * 3,
        out_specs=(vmem, vmem),
        scratch_shapes=[
            pltpu.VMEM((NEW, D), BF16),
            pltpu.VMEM((D, COLS), BF16),
            pltpu.VMEM((2, SHARD, 128), BF16),
            pltpu.VMEM((D, D), BF16),
            pltpu.VMEM((CACHE, 128), BF16),
            pltpu.VMEM((CACHE, 128), BF16),
            pltpu.VMEM((NEW, 128), BF16),
            pltpu.VMEM((RING * QROWS, 128), BF16),
            pltpu.VMEM((RING * QROWS, 128), F32),
            pltpu.VMEM((RING * QROWS, 128), F32),
            pltpu.VMEM((QROWS, CACHE), F32),
            pltpu.VMEM((NEW, 256), BF16),
            pltpu.VMEM((ROWS, D), BF16),
            pltpu.VMEM((NEW, 128), F32),
            pltpu.VMEM((NEW, 128), F32),
            dma((5,)),
            dma((2,)),
            dma((2, STAGES)),
            dma(()),
            dma((RING - 1,)),
            dma((2,)),
            dma((2, len(OFFSETS))),
            dma(()),
            dma(()),
            dma((2,)),
            dma((2, STAGES)),
            dma((2,)),
            dma((2, STAGES // 2)),
            dma(()),
            dma(()),
            dma(()),
            dma(()),
        ],
        compiler_params=pltpu.CompilerParams(
            collective_id=0, has_side_effects=True, vmem_limit_bytes=60 << 20
        ),
        name="prefill",
    )(
        tokens,
        norm_gain.reshape(1, D),
        query_weight,
        keyval_weight,
        query_gain.reshape(1, HD),
        key_gain.reshape(1, HD),
        output_weight,
        keyval_cache,
        inverse_freq,
        cached_lengths,
        sink_count,
        window,
    )


def solution(mesh):
    in_specs = (
        P(("dp", "tensor"), None),
        P(),
        P("dp", None),
        P(None, "dp", None),
        P(),
        P(),
        P(None, "dp"),
        P(("dp", "tensor"), None, None),
        P("dp"),
        P("dp"),
        P("dp"),
    )
    out_specs = (P(("dp", "tensor"), None), P(("dp", "tensor"), None, None))
    return jax.shard_map(body, mesh=mesh, in_specs=in_specs, out_specs=out_specs, check_vma=False)
```
